32 devices in a mesh: comp: 4 (over y, core), tile: 8 (over z, x).
Axes of the slice: x: 2, y: 2, z: 4, core: 2. Of those that a mesh axis runs over, the one named last changes fastest.
Arguments:
- state: float32 [2, 8, 256, 4096], P(None, None, 'comp', 'tile'), may hold values from -6 to 6
- courant: float32 [8, 256], P(None, 'comp'), may hold values from -0.9 to 0.9
- mixing: float32 [7, 256], P(None, 'comp'), may hold values from 0.05 to 0.24
- exchange_coef: float32 [256, 4096], P('comp', 'tile'), may hold values from 0.2 to 0.8
- sea_mask: int32 [256, 4096], P('comp', 'tile'), may hold values 0 or 1
- margin_count: int32 [4, 8, 3, 4], P('comp', 'tile'), may hold values from 0 to 4096, as said below
- margin_row: int32 [4, 8, 3, 4, 4096], P('comp', 'tile'), may hold values from 0 to 63
- margin_col: int32 [4, 8, 3, 4, 4096], P('comp', 'tile'), may hold values from 0 to 511, as said below
- margin_weight: float32 [4, 8, 3, 4, 4096], P('comp', 'tile'), may hold values from 0.05 to 0.6
Outputs:
- new_state: float32 [2, 8, 256, 4096], P(None, None, 'comp', 'tile')
- partner_surface: float32 [2, 256, 4096], P(None, 'comp', 'tile')
The draws below stay inside these ranges and needn't reach their ends.
Inputs may be any that keep to these rules, and one draw needn't show every extreme that they name: margin_count[g, t, o, h] equals margin_count[h, (t + o - 1) mod 8, 2 - o, g], and row r of the one list is the same margin as row r of the other. Only pairs of one atmosphere device (comp index below 3) and one ocean device have rows: an atmosphere device couples with the three ocean devices at tile offsets -1, 0 and 1, an ocean device with the atmosphere devices at those offsets; every such pair has at least 3584 rows. `margin_col`: for list index o = 0 (partner to the west) the columns lie below 128, for o = 2 (partner to the east) at 384 or above.
All inputs are finite; a program needn't handle non-finite values. No bound on the sum of `sea_mask` on one device may be relied on, other than what follows from the above.
Results may differ from the reference program's by a relative error of at most 0.0003.
Values sent between devices are 32-bit elements; how exact they have to be, the bound alone decides.
A program may use at most 64 MiB of HBM per device.

```python
import math
import jax
import jax.numpy as jnp
from jax import lax

NF = 2
LEV = 8
SUBSTEPS = 2
BY = 64
BX = 512
CAP = 4096
ROWS = 256
COLS = 4096
N_COMP = 4
N_TILE = 8


def draw_margin_count(key, part):
    deficit = jax.random.randint(key, (N_COMP - 1, N_TILE, 3), 0, max(CAP // 8, 2))
    base = (CAP - deficit).astype(jnp.int32)
    base = base.at[0, 0, 0].set(CAP)
    full = jnp.zeros((N_COMP, N_TILE, 3, N_COMP), jnp.int32)
    full = full.at[:N_COMP - 1, :, :, N_COMP - 1].set(base)
    tiles = jnp.arange(N_TILE, dtype=jnp.int32)
    for which in range(3):
        source_tile = (tiles + which - 1) % N_TILE
        mirrored = jnp.transpose(base[:, source_tile, 2 - which], (1, 0))
        full = full.at[N_COMP - 1, :, which, :N_COMP - 1].set(mirrored)
    return full


def draw_margin_col(key, part):
    shape = (N_COMP, N_TILE, 3, N_COMP, CAP)
    anywhere = jax.random.randint(key, shape, 0, BX)
    edge = jax.random.randint(jax.random.fold_in(key, 1), shape, 0, BX // 4)
    which = jnp.arange(3, dtype=jnp.int32)[None, None, :, None, None]
    column = jnp.where(which == 0, edge, jnp.where(which == 2, BX - 1 - edge, anywhere))
    column = column.at[0, 0, 1, 0, 0].set(BX - 1)
    column = column.at[0, 0, 1, 0, 1].set(0)
    return column.astype(jnp.int32)


def with_ends(values, key, smallest, high):
    dims = values.shape
    spot = [jax.random.randint(jax.random.fold_in(key, axis), (), 0, dims[axis]) for axis in range(len(dims))]
    values = values.at[tuple(spot)].set(smallest)
    longest = dims.index(max(dims))
    spot[longest] = (spot[longest] + 1) % dims[longest]
    return values.at[tuple(spot)].set(high)


def shard_levels(rng, shape, pieces, least, high):
    def one(position, shards_of):
        heights = jax.random.uniform(jax.random.fold_in(jax.random.fold_in(rng, 6), position), (shards_of,), jnp.float32, least / len(pieces), high / len(pieces))
        return jnp.repeat(jnp.exp(heights), shape[position] // shards_of).reshape((-1,) + (1,) * (len(shape) - position - 1))

    gain = one(*pieces[0])
    for cut in pieces[1:]:
        gain = gain * one(*cut)
    return gain


def noise(stream_key, dims, width, limit, pieces=(), held_as=jnp.bfloat16):
    entries = jax.random.normal(stream_key, dims, jnp.float32) * width
    if len(pieces) > 0:
        entries = shard_levels(stream_key, dims, pieces, -0.22, 0.18) * entries
    return jnp.clip(entries, min=-limit, max=limit).astype(held_as)


def setup_inputs(seed: int = 0) -> dict:
    key_list = jax.random.split(jax.random.key(seed), 10)
    return {
        "state": noise(key_list[0], (NF, LEV, ROWS, COLS), 1.0, 6.0, ((2, 4), (3, 8)), jnp.float32),
        "courant": jnp.clip(jax.random.uniform(key_list[1], (LEV, ROWS), jnp.float32, -0.9, 0.9) * shard_levels(key_list[1], (LEV, ROWS), ((1, 4),), -0.4, 0.0), -0.9, 0.9),
        "mixing": jnp.clip(jnp.exp(math.log(0.24) - 1.5686159 * jax.random.uniform(key_list[2], (LEV - 1, ROWS), jnp.float32) ** shard_levels(key_list[2], (LEV - 1, ROWS), ((1, 4),), -0.2, 0.2)), 0.05, 0.24),
        "exchange_coef": jnp.clip(jnp.exp(math.log(0.8) - 1.3862944 * jax.random.uniform(key_list[3], (ROWS, COLS), jnp.float32) ** shard_levels(key_list[3], (ROWS, COLS), ((0, 4), (1, 8)), -0.2, 0.2)), 0.2, 0.8),
        "sea_mask": with_ends((jax.random.randint(key_list[4], (ROWS, COLS), 0, 4) < 3).astype(jnp.int32), jax.random.fold_in(key_list[4], 1), 0, 1),
        "margin_count": draw_margin_count(jax.random.fold_in(key_list[9], 71), 0),
        "margin_row": with_ends(jax.random.randint(key_list[6], (N_COMP, N_TILE, 3, N_COMP, CAP), 0, BY), jax.random.fold_in(key_list[6], 1), 0, BY - 1).astype(jnp.int32),
        "margin_col": draw_margin_col(jax.random.fold_in(key_list[9], 71), 0),
        "margin_weight": jnp.clip(0.05 + 0.55 * jax.random.uniform(key_list[8], (N_COMP, N_TILE, 3, N_COMP, CAP), jnp.float32) ** shard_levels(key_list[8], (N_COMP, N_TILE, 3, N_COMP, CAP), ((0, 4), (1, 8)), -0.2, 0.2), 0.05, 0.6),
    }


def transport(padded, speed):
    left = padded[..., :-2]
    middle = padded[..., 1:-1]
    right = padded[..., 2:]
    return middle - 0.5 * speed * (right - left) + 0.5 * speed * speed * (right - 2.0 * middle + left)


def vertical_mix(field, coeff):
    jump_up = field[:, 1:] - field[:, :-1]
    flux = coeff[None, :, :, None] * jump_up
    empty = jnp.zeros_like(flux[:, :1])
    upper = jnp.concatenate([flux, empty], axis=1)
    lower = jnp.concatenate([empty, flux], axis=1)
    return field + upper - lower


def reference(state, courant, mixing, exchange_coef, sea_mask, margin_count, margin_row, margin_col, margin_weight):
    devices_all = N_COMP * N_TILE
    cell_count = BY * BX
    surface = state[:, 0].reshape(NF, N_COMP, BY, N_TILE, BX).transpose(1, 3, 0, 2, 4).reshape(N_COMP, N_TILE, NF, cell_count)
    cells_table = (margin_row * BX + margin_col).astype(jnp.int32)
    slots = jnp.arange(CAP, dtype=jnp.int32)
    offsets = jnp.arange(3, dtype=jnp.int32)
    comp_index = jnp.arange(N_COMP, dtype=jnp.int32)[:, None]
    back_index = (2 - offsets)[None, :]

    def receive(index):
        home_comp = index // N_TILE
        home_tile = index % N_TILE
        source_tile = ((home_tile + offsets - 1) % N_TILE)[None, :]
        source_cells = cells_table[comp_index, source_tile, back_index, home_comp]
        source_counts = margin_count[comp_index, source_tile, back_index, home_comp]
        source_surface = surface[comp_index, source_tile]
        values = jnp.take_along_axis(source_surface, source_cells[:, :, None, :], axis=3)
        live = slots[None, None, :] < source_counts[:, :, None]
        values = jnp.where(live[:, :, None, :], values, 0.0)
        weights = jnp.transpose(margin_weight[home_comp, home_tile], (1, 0, 2))
        terms = values * weights[:, :, None, :]
        landing = jnp.transpose(cells_table[home_comp, home_tile], (1, 0, 2)).reshape(-1)
        flat_terms = jnp.transpose(terms, (2, 0, 1, 3)).reshape(NF, -1)
        summed = jnp.zeros((NF, cell_count), jnp.float32)
        return summed.at[:, landing].add(flat_terms)

    received = lax.map(receive, jnp.arange(devices_all, dtype=jnp.int32))
    partner = received.reshape(N_COMP, N_TILE, NF, BY, BX).transpose(2, 0, 3, 1, 4).reshape(NF, N_COMP * BY, N_TILE * BX)

    speed = courant[:, :, None]
    field = state
    for step in range(SUBSTEPS):
        padded = jnp.concatenate([field[..., -1:], field, field[..., :1]], axis=3)
        field = vertical_mix(transport(padded, speed), mixing)

    ocean = (jnp.arange(N_COMP * BY, dtype=jnp.int32) >= (N_COMP - 1) * BY)[:, None]
    rate = exchange_coef * sea_mask.astype(jnp.float32)
    first_own = field[0, 0]
    second_own = field[1, 0]
    first_far = partner[0]
    second_far = partner[1]
    new_first = first_own + rate * (first_far - first_own)
    air_second = second_own + rate * (1.2 * first_far - 0.3 * second_far - second_own)
    sea_second = second_own + rate * (1.2 * first_own - second_far)
    new_second = jnp.where(ocean, sea_second, air_second)
    field = field.at[:, 0].set(jnp.stack([new_first, new_second]))
    return field, partner
```

```python
import functools

import jax
import jax.numpy as jnp
from jax import lax
from jax.experimental import pallas as pl
from jax.experimental.pallas import tpu as pltpu
from jax.sharding import PartitionSpec as P

SUBSTEPS = 2
LANES = 128
MESH = pl.DeviceIdType.MESH
SHIFT = 256


def chunk_of(slot_count):
    for width in (1024, 512, 256):
        if slot_count % width == 0:
            return width
    return slot_count


def one_hot(iota_ref, key, depth):
    width = key.shape[1]
    shifted = (key - SHIFT).astype(jnp.float32)
    wide = jnp.broadcast_to(shifted, (16, width)).astype(jnp.bfloat16)
    one = jnp.ones((16, width), jnp.bfloat16)
    zero = jnp.zeros((16, width), jnp.bfloat16)
    parts = []
    for start in range(0, depth, 16):
        number = iota_ref[start : start + 16, :]
        number = jnp.concatenate([number] * (width // LANES), axis=1)
        parts.append(jnp.where(wide == number, one, zero))
    return jnp.concatenate(parts, axis=0)


def split(values):
    high = values.astype(jnp.bfloat16)
    low = (values - high.astype(jnp.float32)).astype(jnp.bfloat16)
    return high, low


def keys_of(which, row, col, row_count, col_count):
    if which == 1:
        return col, row
    half = row_count // 2
    edge = col_count // 4
    base = 0 if which == 0 else col_count - edge
    upper = (row >= half).astype(jnp.int32)
    return upper * edge + (col - base), row - upper * half


def exchange_kernel(
    row_count,
    col_count,
    slot_count,
    comp_total,
    tile_total,
    fl_count,
    state_ref,
    count_ref,
    row_ref,
    col_ref,
    weight_ref,
    partner_ref,
    halo_ref,
    surface,
    edges,
    table_mid,
    table_side,
    outgoing,
    incoming,
    halo_out,
    halo_in,
    total_mid,
    total_side,
    iota_ref,
    load_sem,
    send_sem,
    recv_sem,
    halo_send_sem,
    halo_recv_sem,
):
    comp = lax.axis_index("comp")
    tile = lax.axis_index("tile")
    ocean = comp == comp_total - 1
    tiles = [lax.rem(tile + offset + tile_total, tile_total) for offset in (-1, 0, 1)]
    fields = surface.shape[0]
    half = row_count // 2
    edge = col_count // 4
    width = chunk_of(slot_count)
    chunks = slot_count // width
    low_list = jnp.where(ocean, 0, comp_total - 1)
    high_list = jnp.where(ocean, comp_total - 1, comp_total)

    load_surface = pltpu.make_async_copy(state_ref.at[:, 0], surface, load_sem.at[0])
    load_surface.start()
    loads = []
    for side, start in ((0, 0), (1, col_count - LANES)):
        load = pltpu.make_async_copy(
            state_ref.at[:, :, :, pl.ds(start, LANES)], edges.at[side], load_sem.at[1 + side]
        )
        load.start()
        loads.append(load)

    barrier = pltpu.get_barrier_semaphore()
    for which in (0, 2):
        pl.semaphore_signal(barrier, inc=1, device_id=(comp, tiles[which]), device_id_type=MESH)

    def greet(other, carry):
        for which in range(3):
            pl.semaphore_signal(
                barrier, inc=1, device_id=(other, tiles[which]), device_id_type=MESH
            )
        return carry

    lax.fori_loop(low_list, high_list, greet, 0)

    iota_ref[...] = (lax.broadcasted_iota(jnp.int32, iota_ref.shape, 0) - SHIFT).astype(
        jnp.float32
    ).astype(jnp.bfloat16)
    load_surface.wait()
    for field in range(fields):
        value = surface[field]
        high, low = split(value)
        for index, piece in ((field, high), (fields + field, low)):
            table_mid[index * row_count : (index + 1) * row_count, :] = piece
            for side, base in ((0, 0), (1, col_count - edge)):
                table_side[side, index * half : (index + 1) * half, :] = jnp.concatenate(
                    [piece[:half, base : base + edge], piece[half:, base : base + edge]], axis=1
                )
    total_mid[...] = jnp.zeros_like(total_mid)
    total_side[...] = jnp.zeros_like(total_side)

    pl.semaphore_wait(barrier, 2 + 3 * (high_list - low_list))

    def copy_of(which, other):
        return pltpu.make_async_remote_copy(
            src_ref=outgoing.at[which, other],
            dst_ref=incoming.at[2 - which, comp],
            send_sem=send_sem.at[which, other],
            recv_sem=recv_sem.at[2 - which, comp],
            device_id=(other, tiles[which]),
            device_id_type=MESH,
        )

    def landing_of(which, other):
        return pltpu.make_async_remote_copy(
            src_ref=outgoing.at[which, other],
            dst_ref=incoming.at[which, other],
            send_sem=send_sem.at[which, other],
            recv_sem=recv_sem.at[which, other],
            device_id=(other, tiles[which]),
            device_id_type=MESH,
        )

    def pick(other, carry):
        for which in (1, 0, 2):
            count = count_ref[which, other]

            def pick_chunk(piece, inner):
                start = pl.multiple_of(piece * width, width)
                span = pl.ds(start, width)
                row = row_ref[which, pl.ds(other, 1), span]
                col = col_ref[which, pl.ds(other, 1), span]
                key, inside = keys_of(which, row, col, row_count, col_count)
                if which == 1:
                    table, depth, rows = table_mid[...], col_count, row_count
                else:
                    table, depth, rows = table_side[which // 2], 2 * edge, half
                picked = jnp.dot(
                    table, one_hot(iota_ref, key, depth), preferred_element_type=jnp.float32
                )
                match = lax.broadcasted_iota(jnp.int32, (rows, width), 0) == inside
                live = lax.broadcasted_iota(jnp.int32, (1, width), 1) + start < count
                for field in range(fields):
                    both = (
                        picked[field * rows : (field + 1) * rows]
                        + picked[(fields + field) * rows : (fields + field + 1) * rows]
                    )
                    value = jnp.sum(jnp.where(match, both, 0.0), axis=0, keepdims=True)
                    outgoing[which, other, field : field + 1, span] = jnp.where(live, value, 0.0)
                return inner

            lax.fori_loop(0, chunks, pick_chunk, 0)
            copy_of(which, other).start()
        return carry

    lax.fori_loop(low_list, high_list, pick, 0)

    for load in loads:
        load.wait()
    lane = lax.broadcasted_iota(jnp.int32, (row_count, LANES), 1)
    for side in range(2):
        packed = jnp.zeros((row_count, LANES), jnp.float32)
        for place in range(fl_count):
            level = edges[side, place // (fl_count // fields), place % (fl_count // fields)]
            shift = SUBSTEPS * place + (0 if side == 0 else SUBSTEPS)
            moved = level if shift == 0 else pltpu.roll(level, shift, 1)
            packed = jnp.where(lane // SUBSTEPS == place, moved, packed)
        halo_out[side] = packed

    def halo_copy(side):
        return pltpu.make_async_remote_copy(
            src_ref=halo_out.at[side],
            dst_ref=halo_in.at[1 - side],
            send_sem=halo_send_sem.at[side],
            recv_sem=halo_recv_sem.at[1 - side],
            device_id=(comp, tiles[2 * side]),
            device_id_type=MESH,
        )

    for side in range(2):
        halo_copy(side).start()

    def land(other, carry):
        for which in (1, 0, 2):
            landing_of(which, other).wait_recv()

            def land_chunk(piece, inner):
                start = pl.multiple_of(piece * width, width)
                span = pl.ds(start, width)
                row = row_ref[which, pl.ds(other, 1), span]
                col = col_ref[which, pl.ds(other, 1), span]
                key, inside = keys_of(which, row, col, row_count, col_count)
                depth, rows = (
                    (col_count, row_count) if which == 1 else (2 * edge, half)
                )
                term = incoming[which, other, :, span] * weight_ref[which, pl.ds(other, 1), span]
                high, low = split(term)
                wide_key = jnp.broadcast_to(
                    inside.astype(jnp.float32) - SHIFT, (16, width)
                ).astype(jnp.bfloat16)
                zero = jnp.zeros((16, width), jnp.bfloat16)
                parts = []
                matches = []
                for first in range(0, rows, 16):
                    number = iota_ref[first : first + 16, :]
                    number = jnp.concatenate([number] * (width // LANES), axis=1)
                    matches.append(wide_key == number)
                for piece_of in (high, low):
                    for field in range(fields):
                        value = jnp.broadcast_to(
                            piece_of[field : field + 1].astype(jnp.float32), (16, width)
                        ).astype(jnp.bfloat16)
                        for match in matches:
                            parts.append(jnp.where(match, value, zero))
                spread = jnp.concatenate(parts, axis=0)
                added = lax.dot_general(
                    spread,
                    one_hot(iota_ref, key, depth),
                    (((1,), (1,)), ((), ())),
                    preferred_element_type=jnp.float32,
                )
                if which == 1:
                    total_mid[...] += added
                else:
                    total_side[which // 2] += added
                return inner

            lax.fori_loop(0, chunks, land_chunk, 0)
        return carry

    lax.fori_loop(low_list, high_list, land, 0)

    for field in range(fields):
        first, second = field, fields + field
        whole = (
            total_mid[first * row_count : (first + 1) * row_count, :]
            + total_mid[second * row_count : (second + 1) * row_count, :]
        )
        partner_ref[field] = whole
        for side, base in ((0, 0), (1, col_count - edge)):
            extra = (
                total_side[side, first * half : (first + 1) * half, :]
                + total_side[side, second * half : (second + 1) * half, :]
            )
            partner_ref[field, :half, base : base + edge] += extra[:, :edge]
            partner_ref[field, half:, base : base + edge] += extra[:, edge:]

    def finish(other, carry):
        for which in range(3):
            copy_of(which, other).wait_send()
        return carry

    lax.fori_loop(low_list, high_list, finish, 0)
    for side in range(2):
        copy = halo_copy(side)
        copy.wait_send()
    for side in range(2):
        halo_copy(1 - side).wait_recv()
        halo_ref[side] = halo_in[side]


def advance_kernel(
    state_ref,
    courant_ref,
    mixing_ref,
    exchange_ref,
    sea_ref,
    halo_ref,
    partner_in_ref,
    new_ref,
    partner_ref,
    speed_ref,
    mix_ref,
):
    fields, levels, rows, cols = state_ref.shape
    step = pl.program_id(0)
    ocean = lax.axis_index("comp") == lax.axis_size("comp") - 1

    @pl.when(step == 0)
    def _():
        speed_ref[...] = jnp.transpose(courant_ref[...])
        mix_ref[...] = jnp.transpose(mixing_ref[...])

    span = pl.ds(pl.multiple_of(step * rows, rows), rows)
    total = cols + LANES
    lane = lax.broadcasted_iota(jnp.int32, (rows, LANES), 1)
    speeds = speed_ref[span, :]
    mixes = mix_ref[span, :]
    surface = []
    for field in range(fields):
        columns = []
        for level in range(levels):
            place = field * levels + level
            east = halo_ref[1]
            east = east if place == 0 else pltpu.roll(east, LANES - SUBSTEPS * place, 1)
            west = pltpu.roll(halo_ref[0], LANES - SUBSTEPS * (place + 1), 1)
            ends = jnp.where(lane < LANES // 2, east, west)
            columns.append(jnp.concatenate([state_ref[field, level], ends], axis=1))
        for substep in range(SUBSTEPS):
            moved = []
            for level in range(levels):
                c = jnp.broadcast_to(speeds[:, level : level + 1], (rows, total))
                q = columns[level]
                left = pltpu.roll(q, 1, 1)
                right = pltpu.roll(q, total - 1, 1)
                moved.append(q - 0.5 * c * (right - left) + 0.5 * c * c * (right - 2.0 * q + left))
            columns = []
            flux = None
            for level in range(levels):
                value = moved[level]
                if level < levels - 1:
                    m = jnp.broadcast_to(mixes[:, level : level + 1], (rows, total))
                    above = m * (moved[level + 1] - moved[level])
                    value = value + above
                if level > 0:
                    value = value - flux
                if level < levels - 1:
                    flux = above
                columns.append(value)
        for level in range(1, levels):
            new_ref[field, level] = columns[level][:, :cols]
        surface.append(columns[0][:, :cols])
    rate = exchange_ref[...] * sea_ref[...].astype(jnp.float32)
    first, second = surface
    far = partner_in_ref[0]
    far_second = partner_in_ref[1]
    new_ref[0, 0] = first + rate * (far - first)
    air = second + rate * (1.2 * far - 0.3 * far_second - second)
    sea = second + rate * (1.2 * first - far_second)
    new_ref[1, 0] = jnp.where(ocean, sea, air)
    partner_ref[...] = partner_in_ref[...]


def shards(
    state,
    courant,
    mixing,
    exchange_coef,
    sea_mask,
    margin_count,
    margin_row,
    margin_col,
    margin_weight,
):
    fields, levels, rows, cols = state.shape
    slots = margin_row.shape[-1]
    comp_total = lax.axis_size("comp")
    tile_total = lax.axis_size("tile")
    half = rows // 2
    edge = cols // 4
    lists = (3, comp_total, slots)
    vmem = pl.BlockSpec(memory_space=pltpu.VMEM)
    partner, halo = pl.pallas_call(
        functools.partial(
            exchange_kernel, rows, cols, slots, comp_total, tile_total, fields * levels
        ),
        out_shape=(
            jax.ShapeDtypeStruct((fields, rows, cols), jnp.float32),
            jax.ShapeDtypeStruct((2, rows, LANES), jnp.float32),
        ),
        in_specs=[
            pl.BlockSpec(memory_space=pl.ANY),
            pl.BlockSpec(memory_space=pltpu.SMEM),
            vmem,
            vmem,
            vmem,
        ],
        out_specs=(vmem, vmem),
        scratch_shapes=[
            pltpu.VMEM((fields, rows, cols), jnp.float32),
            pltpu.VMEM((2, fields, levels, rows, LANES), jnp.float32),
            pltpu.VMEM((2 * fields * rows, cols), jnp.bfloat16),
            pltpu.VMEM((2, 2 * fields * half, 2 * edge), jnp.bfloat16),
            pltpu.VMEM((3, comp_total, fields, slots), jnp.float32),
            pltpu.VMEM((3, comp_total, fields, slots), jnp.float32),
            pltpu.VMEM((2, rows, LANES), jnp.float32),
            pltpu.VMEM((2, rows, LANES), jnp.float32),
            pltpu.VMEM((2 * fields * rows, cols), jnp.float32),
            pltpu.VMEM((2, 2 * fields * half, 2 * edge), jnp.float32),
            pltpu.VMEM((cols, LANES), jnp.bfloat16),
            pltpu.SemaphoreType.DMA((3,)),
            pltpu.SemaphoreType.DMA((3, comp_total)),
            pltpu.SemaphoreType.DMA((3, comp_total)),
            pltpu.SemaphoreType.DMA((2,)),
            pltpu.SemaphoreType.DMA((2,)),
        ],
        compiler_params=pltpu.CompilerParams(
            collective_id=0, has_side_effects=True, vmem_limit_bytes=48 * 1024 * 1024
        ),
    )(
        state,
        margin_count.reshape(3, comp_total),
        margin_row.reshape(lists),
        margin_col.reshape(lists),
        margin_weight.reshape(lists),
    )
    block = 8
    plane = pl.BlockSpec((block, cols), lambda i: (i, 0))
    return pl.pallas_call(
        advance_kernel,
        grid=(rows // block,),
        out_shape=(
            jax.ShapeDtypeStruct(state.shape, jnp.float32),
            jax.ShapeDtypeStruct((fields, rows, cols), jnp.float32),
        ),
        in_specs=[
            pl.BlockSpec((fields, levels, block, cols), lambda i: (0, 0, i, 0)),
            pl.BlockSpec(courant.shape, lambda i: (0, 0)),
            pl.BlockSpec(mixing.shape, lambda i: (0, 0)),
            plane,
            plane,
            pl.BlockSpec((2, block, LANES), lambda i: (0, i, 0)),
            pl.BlockSpec((fields, block, cols), lambda i: (0, i, 0)),
        ],
        out_specs=(
            pl.BlockSpec((fields, levels, block, cols), lambda i: (0, 0, i, 0)),
            pl.BlockSpec((fields, block, cols), lambda i: (0, i, 0)),
        ),
        scratch_shapes=[
            pltpu.VMEM((rows, levels), jnp.float32),
            pltpu.VMEM((rows, levels - 1), jnp.float32),
        ],
    )(state, courant, mixing, exchange_coef, sea_mask, halo, partner)


def solution(mesh):
    in_specs = (
        P(None, None, "comp", "tile"),
        P(None, "comp"),
        P(None, "comp"),
        P("comp", "tile"),
        P("comp", "tile"),
        P("comp", "tile", None, None),
        P("comp", "tile", None, None, None),
        P("comp", "tile", None, None, None),
        P("comp", "tile", None, None, None),
    )
    out_specs = (P(None, None, "comp", "tile"), P(None, "comp", "tile"))
    return jax.shard_map(shards, mesh=mesh, in_specs=in_specs, out_specs=out_specs, check_vma=False)
```

```python
import functools

import jax
import jax.numpy as jnp
from jax import lax
from jax.experimental import pallas as pl
from jax.experimental.pallas import tpu as pltpu
from jax.sharding import PartitionSpec as P

SUBSTEPS = 2
LANES = 128
MESH = pl.DeviceIdType.MESH
SHIFT = 256
VMEM_BYTES = 67043328


def chunk_of(slot_count):
    for width in (1024, 512, 256):
        if slot_count % width == 0:
            return width
    return slot_count


def one_hot(iota_ref, key, depth):
    width = key.shape[1]
    shifted = (key - SHIFT).astype(jnp.float32)
    wide = jnp.broadcast_to(shifted, (16, width)).astype(jnp.bfloat16)
    one = jnp.ones((16, width), jnp.bfloat16)
    zero = jnp.zeros((16, width), jnp.bfloat16)
    parts = []
    for start in range(0, depth, 16):
        number = iota_ref[start : start + 16, :]
        number = jnp.concatenate([number] * (width // LANES), axis=1)
        parts.append(jnp.where(wide == number, one, zero))
    return jnp.concatenate(parts, axis=0)


def split(values):
    high = values.astype(jnp.bfloat16)
    low = (values - high.astype(jnp.float32)).astype(jnp.bfloat16)
    return high, low


def keys_of(which, row, col, row_count, col_count):
    if which == 1:
        return col, row
    half = row_count // 2
    edge = col_count // 4
    base = 0 if which == 0 else col_count - edge
    upper = (row >= half).astype(jnp.int32)
    return upper * edge + (col - base), row - upper * half


def exchange_kernel(
    row_count,
    col_count,
    slot_count,
    comp_total,
    tile_total,
    fl_count,
    state_ref,
    count_ref,
    row_hbm,
    col_hbm,
    weight_hbm,
    partner_hbm,
    halo_ref,
    row_ref,
    col_ref,
    weight_ref,
    partner_ref,
    surface,
    edges,
    table_mid,
    table_side,
    outgoing,
    incoming,
    halo_out,
    total_mid,
    total_side,
    iota_ref,
    load_sem,
    send_sem,
    recv_sem,
    halo_send_sem,
    halo_recv_sem,
):
    comp = lax.axis_index("comp")
    tile = lax.axis_index("tile")
    ocean = comp == comp_total - 1
    tiles = [lax.rem(tile + offset + tile_total, tile_total) for offset in (-1, 0, 1)]
    fields = surface.shape[0]
    half = row_count // 2
    edge = col_count // 4
    width = chunk_of(slot_count)
    chunks = slot_count // width
    low_list = jnp.where(ocean, 0, comp_total - 1)
    high_list = jnp.where(ocean, comp_total - 1, comp_total)

    load_surface = pltpu.make_async_copy(state_ref.at[:, 0], surface, load_sem.at[0])
    load_surface.start()
    list_loads = []
    for place, (source, target) in enumerate(
        ((row_hbm, row_ref), (col_hbm, col_ref), (weight_hbm, weight_ref))
    ):
        load = pltpu.make_async_copy(source, target, load_sem.at[3 + place])
        load.start()
        list_loads.append(load)
    loads = []
    for side, start in ((0, 0), (1, col_count - LANES)):
        load = pltpu.make_async_copy(
            state_ref.at[:, :, :, pl.ds(start, LANES)], edges.at[side], load_sem.at[1 + side]
        )
        load.start()
        loads.append(load)

    barrier = pltpu.get_barrier_semaphore()
    for which in (0, 2):
        pl.semaphore_signal(barrier, inc=1, device_id=(comp, tiles[which]), device_id_type=MESH)

    def greet(other, carry):
        for which in range(3):
            pl.semaphore_signal(
                barrier, inc=1, device_id=(other, tiles[which]), device_id_type=MESH
            )
        return carry

    lax.fori_loop(low_list, high_list, greet, 0)

    iota_ref[...] = (lax.broadcasted_iota(jnp.int32, iota_ref.shape, 0) - SHIFT).astype(
        jnp.float32
    ).astype(jnp.bfloat16)
    load_surface.wait()
    for field in range(fields):
        value = surface[field]
        high, low = split(value)
        for index, piece in ((field, high), (fields + field, low)):
            table_mid[index * row_count : (index + 1) * row_count, :] = piece
            for side, base in ((0, 0), (1, col_count - edge)):
                table_side[side, index * half : (index + 1) * half, :] = jnp.concatenate(
                    [piece[:half, base : base + edge], piece[half:, base : base + edge]], axis=1
                )
    total_mid[...] = jnp.zeros_like(total_mid)
    total_side[...] = jnp.zeros_like(total_side)

    for load in list_loads:
        load.wait()
    pl.semaphore_wait(barrier, 2 + 3 * (high_list - low_list))

    def copy_of(which, other):
        return pltpu.make_async_remote_copy(
            src_ref=outgoing.at[which, other],
            dst_ref=incoming.at[2 - which, comp],
            send_sem=send_sem.at[which, other],
            recv_sem=recv_sem.at[2 - which, comp],
            device_id=(other, tiles[which]),
            device_id_type=MESH,
        )

    def landing_of(which, other):
        return pltpu.make_async_remote_copy(
            src_ref=outgoing.at[which, other],
            dst_ref=incoming.at[which, other],
            send_sem=send_sem.at[which, other],
            recv_sem=recv_sem.at[which, other],
            device_id=(other, tiles[which]),
            device_id_type=MESH,
        )

    def pick(other, carry):
        def pick_chunk(piece, inner):
            start = pl.multiple_of(piece * width, width)
            span = pl.ds(start, width)
            live_slot = lax.broadcasted_iota(jnp.int32, (1, width), 1) + start
            for which in (1, 0, 2):
                row = row_ref[which, pl.ds(other, 1), span]
                col = col_ref[which, pl.ds(other, 1), span]
                key, inside = keys_of(which, row, col, row_count, col_count)
                if which == 1:
                    table, depth, rows = table_mid[...], col_count, row_count
                else:
                    table, depth, rows = table_side[which // 2], 2 * edge, half
                picked = jnp.dot(
                    table, one_hot(iota_ref, key, depth), preferred_element_type=jnp.float32
                )
                match = lax.broadcasted_iota(jnp.int32, (rows, width), 0) == inside
                live = live_slot < count_ref[which, 0, other]
                for field in range(fields):
                    both = (
                        picked[field * rows : (field + 1) * rows]
                        + picked[(fields + field) * rows : (fields + field + 1) * rows]
                    )
                    value = jnp.sum(jnp.where(match, both, 0.0), axis=0, keepdims=True)
                    outgoing[which, other, field : field + 1, span] = jnp.where(live, value, 0.0)
            return inner

        lax.fori_loop(0, chunks, pick_chunk, 0)
        for which in range(3):
            copy_of(which, other).start()
        return carry

    lax.fori_loop(low_list, high_list, pick, 0)

    for load in loads:
        load.wait()
    lane = lax.broadcasted_iota(jnp.int32, (row_count, LANES), 1)
    for side in range(2):
        packed = jnp.zeros((row_count, LANES), jnp.float32)
        for place in range(fl_count):
            level = edges[side, place // (fl_count // fields), place % (fl_count // fields)]
            shift = SUBSTEPS * place + (0 if side == 0 else SUBSTEPS)
            moved = level if shift == 0 else pltpu.roll(level, shift, 1)
            packed = jnp.where(lane // SUBSTEPS == place, moved, packed)
        halo_out[side] = packed

    def halo_copy(side):
        return pltpu.make_async_remote_copy(
            src_ref=halo_out.at[side],
            dst_ref=halo_ref.at[1 - side],
            send_sem=halo_send_sem.at[side],
            recv_sem=halo_recv_sem.at[1 - side],
            device_id=(comp, tiles[2 * side]),
            device_id_type=MESH,
        )

    for side in range(2):
        halo_copy(side).start()

    def land(other, carry):
        for which in range(3):
            landing_of(which, other).wait_recv()

        def land_chunk(piece, inner):
            start = pl.multiple_of(piece * width, width)
            span = pl.ds(start, width)
            for which in (1, 0, 2):
                row = row_ref[which, pl.ds(other, 1), span]
                col = col_ref[which, pl.ds(other, 1), span]
                key, inside = keys_of(which, row, col, row_count, col_count)
                depth, rows = (col_count, row_count) if which == 1 else (2 * edge, half)
                term = incoming[which, other, :, span] * weight_ref[which, pl.ds(other, 1), span]
                high, low = split(term)
                wide_key = jnp.broadcast_to(
                    inside.astype(jnp.float32) - SHIFT, (16, width)
                ).astype(jnp.bfloat16)
                zero = jnp.zeros((16, width), jnp.bfloat16)
                parts = []
                matches = []
                for first in range(0, rows, 16):
                    number = iota_ref[first : first + 16, :]
                    number = jnp.concatenate([number] * (width // LANES), axis=1)
                    matches.append(wide_key == number)
                for piece_of in (high, low):
                    for field in range(fields):
                        value = jnp.broadcast_to(
                            piece_of[field : field + 1].astype(jnp.float32), (16, width)
                        ).astype(jnp.bfloat16)
                        for match in matches:
                            parts.append(jnp.where(match, value, zero))
                spread = jnp.concatenate(parts, axis=0)
                added = lax.dot_general(
                    spread,
                    one_hot(iota_ref, key, depth),
                    (((1,), (1,)), ((), ())),
                    preferred_element_type=jnp.float32,
                )
                if which == 1:
                    total_mid[...] += added
                else:
                    total_side[which // 2] += added
            return inner

        lax.fori_loop(0, chunks, land_chunk, 0)
        return carry

    lax.fori_loop(low_list, high_list, land, 0)

    for field in range(fields):
        first, second = field, fields + field
        whole = (
            total_mid[first * row_count : (first + 1) * row_count, :]
            + total_mid[second * row_count : (second + 1) * row_count, :]
        )
        partner_ref[field] = whole
        for side, base in ((0, 0), (1, col_count - edge)):
            extra = (
                total_side[side, first * half : (first + 1) * half, :]
                + total_side[side, second * half : (second + 1) * half, :]
            )
            partner_ref[field, :half, base : base + edge] += extra[:, :edge]
            partner_ref[field, half:, base : base + edge] += extra[:, edge:]
        pltpu.make_async_copy(
            partner_ref.at[field], partner_hbm.at[field], load_sem.at[field]
        ).start()

    def finish(other, carry):
        for which in range(3):
            copy_of(which, other).wait_send()
        return carry

    lax.fori_loop(low_list, high_list, finish, 0)
    for side in range(2):
        copy = halo_copy(side)
        copy.wait_send()
    for side in range(2):
        halo_copy(1 - side).wait_recv()
    for field in range(fields):
        pltpu.make_async_copy(
            partner_ref.at[field], partner_hbm.at[field], load_sem.at[field]
        ).wait()


def advance_kernel(
    state_ref,
    courant_ref,
    mixing_ref,
    exchange_ref,
    sea_ref,
    halo_ref,
    partner_in_ref,
    new_ref,
    partner_ref,
    speed_ref,
    mix_ref,
):
    fields, levels, rows, cols = state_ref.shape
    step = pl.program_id(0)
    ocean = lax.axis_index("comp") == lax.axis_size("comp") - 1

    @pl.when(step == 0)
    def _():
        speed_ref[...] = jnp.transpose(courant_ref[...])
        mix_ref[...] = jnp.transpose(mixing_ref[...])

    span = pl.ds(pl.multiple_of(step * rows, rows), rows)
    total = cols + LANES
    lane = lax.broadcasted_iota(jnp.int32, (rows, LANES), 1)
    speeds = speed_ref[span, :]
    mixes = mix_ref[span, :]
    surface = []
    for field in range(fields):
        columns = []
        for level in range(levels):
            place = field * levels + level
            east = halo_ref[1]
            east = east if place == 0 else pltpu.roll(east, LANES - SUBSTEPS * place, 1)
            west = pltpu.roll(halo_ref[0], LANES - SUBSTEPS * (place + 1), 1)
            ends = jnp.where(lane < LANES // 2, east, west)
            columns.append(jnp.concatenate([state_ref[field, level], ends], axis=1))
        for substep in range(SUBSTEPS):
            moved = []
            for level in range(levels):
                c = jnp.broadcast_to(speeds[:, level : level + 1], (rows, total))
                q = columns[level]
                left = pltpu.roll(q, 1, 1)
                right = pltpu.roll(q, total - 1, 1)
                moved.append(q - 0.5 * c * (right - left) + 0.5 * c * c * (right - 2.0 * q + left))
            columns = []
            flux = None
            for level in range(levels):
                value = moved[level]
                if level < levels - 1:
                    m = jnp.broadcast_to(mixes[:, level : level + 1], (rows, total))
                    above = m * (moved[level + 1] - moved[level])
                    value = value + above
                if level > 0:
                    value = value - flux
                if level < levels - 1:
                    flux = above
                columns.append(value)
        for level in range(1, levels):
            new_ref[field, level] = columns[level][:, :cols]
        surface.append(columns[0][:, :cols])
    rate = exchange_ref[...] * sea_ref[...].astype(jnp.float32)
    first, second = surface
    far = partner_in_ref[0]
    far_second = partner_in_ref[1]
    new_ref[0, 0] = first + rate * (far - first)
    air = second + rate * (1.2 * far - 0.3 * far_second - second)
    sea = second + rate * (1.2 * first - far_second)
    new_ref[1, 0] = jnp.where(ocean, sea, air)
    partner_ref[...] = partner_in_ref[...]


def shards(
    state,
    courant,
    mixing,
    exchange_coef,
    sea_mask,
    margin_count,
    margin_row,
    margin_col,
    margin_weight,
):
    fields, levels, rows, cols = state.shape
    slots = margin_row.shape[-1]
    comp_total = lax.axis_size("comp")
    tile_total = lax.axis_size("tile")
    half = rows // 2
    edge = cols // 4
    lists = (3, comp_total, slots)
    hbm = pl.BlockSpec(memory_space=pl.ANY)
    partner, halo = pl.pallas_call(
        functools.partial(
            exchange_kernel, rows, cols, slots, comp_total, tile_total, fields * levels
        ),
        out_shape=(
            jax.ShapeDtypeStruct((fields, rows, cols), jnp.float32),
            jax.ShapeDtypeStruct((2, rows, LANES), jnp.float32),
        ),
        in_specs=[
            pl.BlockSpec(memory_space=pl.ANY),
            pl.BlockSpec(memory_space=pltpu.SMEM),
            hbm,
            hbm,
            hbm,
        ],
        out_specs=(hbm, hbm),
        scratch_shapes=[
            pltpu.VMEM(lists, jnp.int32),
            pltpu.VMEM(lists, jnp.int32),
            pltpu.VMEM(lists, jnp.float32),
            pltpu.VMEM((fields, rows, cols), jnp.float32),
            pltpu.VMEM((fields, rows, cols), jnp.float32),
            pltpu.VMEM((2, fields, levels, rows, LANES), jnp.float32),
            pltpu.VMEM((2 * fields * rows, cols), jnp.bfloat16),
            pltpu.VMEM((2, 2 * fields * half, 2 * edge), jnp.bfloat16),
            pltpu.VMEM((3, comp_total, fields, slots), jnp.float32),
            pltpu.VMEM((3, comp_total, fields, slots), jnp.float32),
            pltpu.VMEM((2, rows, LANES), jnp.float32),
            pltpu.VMEM((2 * fields * rows, cols), jnp.float32),
            pltpu.VMEM((2, 2 * fields * half, 2 * edge), jnp.float32),
            pltpu.VMEM((cols, LANES), jnp.bfloat16),
            pltpu.SemaphoreType.DMA((6,)),
            pltpu.SemaphoreType.DMA((3, comp_total)),
            pltpu.SemaphoreType.DMA((3, comp_total)),
            pltpu.SemaphoreType.DMA((2,)),
            pltpu.SemaphoreType.DMA((2,)),
        ],
        compiler_params=pltpu.CompilerParams(
            collective_id=0, has_side_effects=True, vmem_limit_bytes=VMEM_BYTES
        ),
    )(
        state,
        margin_count.reshape(3, 1, comp_total),
        margin_row.reshape(lists),
        margin_col.reshape(lists),
        margin_weight.reshape(lists),
    )
    block = 8
    plane = pl.BlockSpec((block, cols), lambda i: (i, 0))
    return pl.pallas_call(
        advance_kernel,
        grid=(rows // block,),
        out_shape=(
            jax.ShapeDtypeStruct(state.shape, jnp.float32),
            jax.ShapeDtypeStruct((fields, rows, cols), jnp.float32),
        ),
        in_specs=[
            pl.BlockSpec((fields, levels, block, cols), lambda i: (0, 0, i, 0)),
            pl.BlockSpec(courant.shape, lambda i: (0, 0)),
            pl.BlockSpec(mixing.shape, lambda i: (0, 0)),
            plane,
            plane,
            pl.BlockSpec((2, block, LANES), lambda i: (0, i, 0)),
            pl.BlockSpec((fields, block, cols), lambda i: (0, i, 0)),
        ],
        out_specs=(
            pl.BlockSpec((fields, levels, block, cols), lambda i: (0, 0, i, 0)),
            pl.BlockSpec((fields, block, cols), lambda i: (0, i, 0)),
        ),
        scratch_shapes=[
            pltpu.VMEM((rows, levels), jnp.float32),
            pltpu.VMEM((rows, levels - 1), jnp.float32),
        ],
    )(state, courant, mixing, exchange_coef, sea_mask, halo, partner)


def solution(mesh):
    in_specs = (
        P(None, None, "comp", "tile"),
        P(None, "comp"),
        P(None, "comp"),
        P("comp", "tile"),
        P("comp", "tile"),
        P("comp", "tile", None, None),
        P("comp", "tile", None, None, None),
        P("comp", "tile", None, None, None),
        P("comp", "tile", None, None, None),
    )
    out_specs = (P(None, None, "comp", "tile"), P(None, "comp", "tile"))
    return jax.shard_map(shards, mesh=mesh, in_specs=in_specs, out_specs=out_specs, check_vma=False)
```

```python
import functools

import jax
import jax.numpy as jnp
from jax import lax
from jax.experimental import pallas as pl
from jax.experimental.pallas import tpu as pltpu
from jax.sharding import PartitionSpec as P

SUBSTEPS = 2
LANES = 128
MESH = pl.DeviceIdType.MESH
SHIFT = 256
VMEM_BYTES = 67043328


def chunk_of(slot_count):
    for width in (2048, 1024, 512, 256):
        if slot_count % width == 0:
            return width
    return slot_count


def one_hot(iota_ref, key, depth):
    width = key.shape[1]
    shifted = (key - SHIFT).astype(jnp.float32)
    wide = jnp.broadcast_to(shifted, (16, width)).astype(jnp.bfloat16)
    one = jnp.ones((16, width), jnp.bfloat16)
    zero = jnp.zeros((16, width), jnp.bfloat16)
    parts = []
    for start in range(0, depth, 16):
        number = iota_ref[start : start + 16, :]
        number = jnp.concatenate([number] * (width // LANES), axis=1)
        parts.append(jnp.where(wide == number, one, zero))
    return jnp.concatenate(parts, axis=0)


def split(values):
    high = values.astype(jnp.bfloat16)
    low = (values - high.astype(jnp.float32)).astype(jnp.bfloat16)
    return high, low


def keys_of(which, row, col, row_count, col_count):
    if which == 1:
        return col, row
    half = row_count // 2
    edge = col_count // 4
    base = 0 if which == 0 else col_count - edge
    upper = (row >= half).astype(jnp.int32)
    return upper * edge + (col - base), row - upper * half


def exchange_kernel(
    row_count,
    col_count,
    slot_count,
    comp_total,
    tile_total,
    fl_count,
    state_ref,
    count_ref,
    row_hbm,
    col_hbm,
    weight_hbm,
    partner_hbm,
    halo_ref,
    row_ref,
    col_ref,
    weight_ref,
    partner_ref,
    surface,
    edges,
    table_mid,
    table_side,
    outgoing,
    incoming,
    halo_out,
    total_mid,
    total_side,
    iota_ref,
    far_surface,
    far_row,
    far_col,
    far_weight,
    far_mid,
    far_side,
    share_out,
    share_in,
    load_sem,
    send_sem,
    recv_sem,
    halo_send_sem,
    halo_recv_sem,
    far_send_sem,
    far_recv_sem,
):
    comp = lax.axis_index("comp")
    tile = lax.axis_index("tile")
    sea = comp_total - 1
    aide = comp_total - 2
    ocean = comp == sea
    helper = comp == aide
    tiles = [lax.rem(tile + offset + tile_total, tile_total) for offset in (-1, 0, 1)]
    fields = surface.shape[0]
    half = row_count // 2
    edge = col_count // 4
    width = chunk_of(slot_count)
    chunks = slot_count // width
    low_list = jnp.where(ocean, 0, sea)
    high_list = jnp.where(ocean, aide, comp_total)
    low_greet = jnp.where(helper, sea, low_list)
    high_greet = jnp.where(helper, sea, high_list)

    load_surface = pltpu.make_async_copy(state_ref.at[:, 0], surface, load_sem.at[0])
    load_surface.start()
    list_loads = []
    for place, (source, target) in enumerate(
        ((row_hbm, row_ref), (col_hbm, col_ref), (weight_hbm, weight_ref))
    ):
        load = pltpu.make_async_copy(source, target, load_sem.at[3 + place])
        load.start()
        list_loads.append(load)
    loads = []
    for side, start in ((0, 0), (1, col_count - LANES)):
        load = pltpu.make_async_copy(
            state_ref.at[:, :, :, pl.ds(start, LANES)], edges.at[side], load_sem.at[1 + side]
        )
        load.start()
        loads.append(load)

    barrier = pltpu.get_barrier_semaphore()
    for which in (0, 2):
        pl.semaphore_signal(barrier, inc=1, device_id=(comp, tiles[which]), device_id_type=MESH)

    def greet(other, carry):
        for which in range(3):
            pl.semaphore_signal(
                barrier, inc=1, device_id=(other, tiles[which]), device_id_type=MESH
            )
        return carry

    lax.fori_loop(low_greet, high_greet, greet, 0)

    @pl.when(ocean)
    def _():
        pl.semaphore_signal(barrier, inc=1, device_id=(aide, tile), device_id_type=MESH)

    @pl.when(helper)
    def _():
        pl.semaphore_signal(barrier, inc=1, device_id=(sea, tile), device_id_type=MESH)

    iota_ref[...] = (lax.broadcasted_iota(jnp.int32, iota_ref.shape, 0) - SHIFT).astype(
        jnp.float32
    ).astype(jnp.bfloat16)
    load_surface.wait()

    def build_tables(source, mid, side_tables):
        for field in range(fields):
            high, low = split(source[field])
            for index, piece in ((field, high), (fields + field, low)):
                mid[index * row_count : (index + 1) * row_count, :] = piece
                for side, base in ((0, 0), (1, col_count - edge)):
                    side_tables[side, index * half : (index + 1) * half, :] = jnp.concatenate(
                        [piece[:half, base : base + edge], piece[half:, base : base + edge]],
                        axis=1,
                    )

    build_tables(surface, table_mid, table_side)
    for load in list_loads:
        load.wait()
    pl.semaphore_wait(
        barrier,
        2 + 3 * (high_greet - low_greet) + jnp.where(ocean | helper, 1, 0),
    )

    far_copies = []
    for place, (source, target) in enumerate(
        (
            (surface, far_surface),
            (row_ref, far_row),
            (col_ref, far_col),
            (weight_ref, far_weight),
        )
    ):
        far_copies.append(
            pltpu.make_async_remote_copy(
                src_ref=source,
                dst_ref=target,
                send_sem=far_send_sem.at[place],
                recv_sem=far_recv_sem.at[place],
                device_id=(aide, tile),
                device_id_type=MESH,
            )
        )
    share_copy = pltpu.make_async_remote_copy(
        src_ref=share_out,
        dst_ref=share_in,
        send_sem=far_send_sem.at[4],
        recv_sem=far_recv_sem.at[4],
        device_id=(sea, tile),
        device_id_type=MESH,
    )

    @pl.when(ocean)
    def _():
        for copy in far_copies:
            copy.start()

    def copy_of(which, other):
        return pltpu.make_async_remote_copy(
            src_ref=outgoing.at[which, other],
            dst_ref=incoming.at[2 - which, comp],
            send_sem=send_sem.at[which, other],
            recv_sem=recv_sem.at[2 - which, comp],
            device_id=(jnp.where(helper, aide, other), tiles[which]),
            device_id_type=MESH,
        )

    def aide_copy(which):
        return pltpu.make_async_remote_copy(
            src_ref=outgoing.at[which, aide],
            dst_ref=incoming.at[2 - which, sea],
            send_sem=send_sem.at[which, aide],
            recv_sem=recv_sem.at[2 - which, sea],
            device_id=(aide, tiles[which]),
            device_id_type=MESH,
        )

    def own_copy(place, source, target):
        return pltpu.make_async_copy(
            outgoing.at[1, source], incoming.at[1, target], load_sem.at[3 + place]
        )

    def landing_of(which, other):
        return pltpu.make_async_remote_copy(
            src_ref=outgoing.at[which, other],
            dst_ref=incoming.at[which, other],
            send_sem=send_sem.at[which, other],
            recv_sem=recv_sem.at[which, other],
            device_id=(other, tiles[which]),
            device_id_type=MESH,
        )

    def pick_lists(other, rows_of, cols_of, mid, side_tables, masked):
        def pick_chunk(piece, inner):
            start = pl.multiple_of(piece * width, width)
            span = pl.ds(start, width)
            live_slot = lax.broadcasted_iota(jnp.int32, (1, width), 1) + start
            for which in (1, 0, 2):
                row = rows_of[which, pl.ds(other, 1), span]
                col = cols_of[which, pl.ds(other, 1), span]
                key, inside = keys_of(which, row, col, row_count, col_count)
                if which == 1:
                    table, depth, rows = mid[...], col_count, row_count
                else:
                    table, depth, rows = side_tables[which // 2], 2 * edge, half
                picked = jnp.dot(
                    table, one_hot(iota_ref, key, depth), preferred_element_type=jnp.float32
                )
                match = lax.broadcasted_iota(jnp.int32, (rows, width), 0) == inside
                if masked:
                    live = live_slot < count_ref[which, 0, other]
                for field in range(fields):
                    both = (
                        picked[field * rows : (field + 1) * rows]
                        + picked[(fields + field) * rows : (fields + field + 1) * rows]
                    )
                    value = jnp.sum(jnp.where(match, both, 0.0), axis=0, keepdims=True)
                    if masked:
                        value = jnp.where(live, value, 0.0)
                    outgoing[which, other, field : field + 1, span] = value
            return inner

        lax.fori_loop(0, chunks, pick_chunk, 0)

    def pick(other, carry):
        pick_lists(other, row_ref, col_ref, table_mid, table_side, True)
        for which in (0, 2):
            copy_of(which, other).start()

        @pl.when(jnp.logical_not(helper))
        def _():
            copy_of(1, other).start()

        return carry

    lax.fori_loop(low_list, high_list, pick, 0)

    @pl.when(helper)
    def _():
        own_copy(0, sea, aide).start()
        for copy in far_copies:
            copy.wait_recv()
        build_tables(far_surface, far_mid, far_side)
        pick_lists(aide, far_row, far_col, far_mid, far_side, False)
        for which in (0, 2):
            aide_copy(which).start()
        own_copy(1, aide, sea).start()

    for load in loads:
        load.wait()
    lane = lax.broadcasted_iota(jnp.int32, (row_count, LANES), 1)
    for side in range(2):
        packed = jnp.zeros((row_count, LANES), jnp.float32)
        for place in range(fl_count):
            level = edges[side, place // (fl_count // fields), place % (fl_count // fields)]
            shift = SUBSTEPS * place + (0 if side == 0 else SUBSTEPS)
            moved = level if shift == 0 else pltpu.roll(level, shift, 1)
            packed = jnp.where(lane // SUBSTEPS == place, moved, packed)
        halo_out[side] = packed

    def halo_copy(side):
        return pltpu.make_async_remote_copy(
            src_ref=halo_out.at[side],
            dst_ref=halo_ref.at[1 - side],
            send_sem=halo_send_sem.at[side],
            recv_sem=halo_recv_sem.at[1 - side],
            device_id=(comp, tiles[2 * side]),
            device_id_type=MESH,
        )

    for side in range(2):
        halo_copy(side).start()

    def land_lists(other, rows_of, cols_of, weights_of, masked):
        def land_chunk(piece, inner):
            start = pl.multiple_of(piece * width, width)
            span = pl.ds(start, width)
            live_slot = lax.broadcasted_iota(jnp.int32, (1, width), 1) + start
            for which in (1, 0, 2):
                row = rows_of[which, pl.ds(other, 1), span]
                col = cols_of[which, pl.ds(other, 1), span]
                key, inside = keys_of(which, row, col, row_count, col_count)
                depth, rows = (col_count, row_count) if which == 1 else (2 * edge, half)
                term = incoming[which, other, :, span] * weights_of[which, pl.ds(other, 1), span]
                if masked:
                    term = jnp.where(live_slot < count_ref[which, 0, other], term, 0.0)
                high, low = split(term)
                wide_key = jnp.broadcast_to(
                    inside.astype(jnp.float32) - SHIFT, (16, width)
                ).astype(jnp.bfloat16)
                zero = jnp.zeros((16, width), jnp.bfloat16)
                parts = []
                matches = []
                for first in range(0, rows, 16):
                    number = iota_ref[first : first + 16, :]
                    number = jnp.concatenate([number] * (width // LANES), axis=1)
                    matches.append(wide_key == number)
                for piece_of in (high, low):
                    for field in range(fields):
                        value = jnp.broadcast_to(
                            piece_of[field : field + 1].astype(jnp.float32), (16, width)
                        ).astype(jnp.bfloat16)
                        for match in matches:
                            parts.append(jnp.where(match, value, zero))
                spread = jnp.concatenate(parts, axis=0)
                added = lax.dot_general(
                    spread,
                    one_hot(iota_ref, key, depth),
                    (((1,), (1,)), ((), ())),
                    preferred_element_type=jnp.float32,
                )
                if which == 1:
                    total_mid[...] += added
                else:
                    total_side[which // 2] += added
            return inner

        lax.fori_loop(0, chunks, land_chunk, 0)

    def land(other, carry):
        for which in (0, 2):
            landing_of(which, other).wait_recv()

        @pl.when(jnp.logical_not(helper))
        def _():
            landing_of(1, other).wait_recv()

        land_lists(other, row_ref, col_ref, weight_ref, True)
        return carry

    def clear_totals():
        total_mid[...] = jnp.zeros_like(total_mid)
        total_side[...] = jnp.zeros_like(total_side)

    def gather_totals(field, target):
        first, second = field, fields + field
        target[field] = (
            total_mid[first * row_count : (first + 1) * row_count, :]
            + total_mid[second * row_count : (second + 1) * row_count, :]
        )
        for side, base in ((0, 0), (1, col_count - edge)):
            extra = (
                total_side[side, first * half : (first + 1) * half, :]
                + total_side[side, second * half : (second + 1) * half, :]
            )
            target[field, :half, base : base + edge] += extra[:, :edge]
            target[field, half:, base : base + edge] += extra[:, edge:]

    clear_totals()

    @pl.when(helper)
    def _():
        own_copy(0, sea, aide).wait()
        for which in (0, 2):
            landing_of(which, aide).wait_recv()
        land_lists(aide, far_row, far_col, far_weight, False)
        for field in range(fields):
            gather_totals(field, share_out)
        share_copy.start()
        clear_totals()
        own_copy(1, aide, sea).wait()

    lax.fori_loop(low_list, high_list, land, 0)

    for field in range(fields):
        gather_totals(field, partner_ref)

    @pl.when(ocean)
    def _():
        share_copy.wait_recv()
        partner_ref[...] += share_in[...]

    for field in range(fields):
        pltpu.make_async_copy(
            partner_ref.at[field], partner_hbm.at[field], load_sem.at[field]
        ).start()

    def finish(other, carry):
        for which in (0, 2):
            copy_of(which, other).wait_send()

        @pl.when(jnp.logical_not(helper))
        def _():
            copy_of(1, other).wait_send()

        return carry

    lax.fori_loop(low_list, high_list, finish, 0)

    @pl.when(helper)
    def _():
        for which in (0, 2):
            aide_copy(which).wait_send()
        share_copy.wait_send()

    @pl.when(ocean)
    def _():
        for copy in far_copies:
            copy.wait_send()

    for side in range(2):
        copy = halo_copy(side)
        copy.wait_send()
    for side in range(2):
        halo_copy(1 - side).wait_recv()
    for field in range(fields):
        pltpu.make_async_copy(
            partner_ref.at[field], partner_hbm.at[field], load_sem.at[field]
        ).wait()


def advance_kernel(
    state_ref,
    courant_ref,
    mixing_ref,
    exchange_ref,
    sea_ref,
    halo_ref,
    partner_in_ref,
    new_ref,
    partner_ref,
    speed_ref,
    mix_ref,
):
    fields, levels, rows, cols = state_ref.shape
    step = pl.program_id(0)
    ocean = lax.axis_index("comp") == lax.axis_size("comp") - 1

    @pl.when(step == 0)
    def _():
        speed_ref[...] = jnp.transpose(courant_ref[...])
        mix_ref[...] = jnp.transpose(mixing_ref[...])

    span = pl.ds(pl.multiple_of(step * rows, rows), rows)
    total = cols + LANES
    lane = lax.broadcasted_iota(jnp.int32, (rows, LANES), 1)
    speeds = speed_ref[span, :]
    mixes = mix_ref[span, :]
    surface = []
    for field in range(fields):
        columns = []
        for level in range(levels):
            place = field * levels + level
            east = halo_ref[1]
            east = east if place == 0 else pltpu.roll(east, LANES - SUBSTEPS * place, 1)
            west = pltpu.roll(halo_ref[0], LANES - SUBSTEPS * (place + 1), 1)
            ends = jnp.where(lane < LANES // 2, east, west)
            columns.append(jnp.concatenate([state_ref[field, level], ends], axis=1))
        for substep in range(SUBSTEPS):
            span_out = total if substep < SUBSTEPS - 1 else cols
            moved = []
            for level in range(levels):
                q = columns[level]
                left = pltpu.roll(q, 1, 1)[:, :span_out]
                right = pltpu.roll(q, total - 1, 1)[:, :span_out]
                c = speeds[:, level : level + 1]
                half_c = 0.5 * c
                half_square = half_c * c
                from_left = jnp.broadcast_to(half_c + half_square, (rows, span_out))
                from_right = jnp.broadcast_to(half_square - half_c, (rows, span_out))
                own = jnp.broadcast_to(1.0 - 2.0 * half_square, (rows, span_out))
                moved.append(own * q[:, :span_out] + from_left * left + from_right * right)
            columns = []
            flux = None
            for level in range(levels):
                value = moved[level]
                if level < levels - 1:
                    m = jnp.broadcast_to(mixes[:, level : level + 1], (rows, span_out))
                    above = m * (moved[level + 1] - moved[level])
                    value = value + above
                if level > 0:
                    value = value - flux
                if level < levels - 1:
                    flux = above
                columns.append(value)
        for level in range(1, levels):
            new_ref[field, level] = columns[level]
        surface.append(columns[0])
    rate = exchange_ref[...] * sea_ref[...].astype(jnp.float32)
    first, second = surface
    far = partner_in_ref[0]
    far_second = partner_in_ref[1]
    new_ref[0, 0] = first + rate * (far - first)
    air = second + rate * (1.2 * far - 0.3 * far_second - second)
    sea = second + rate * (1.2 * first - far_second)
    new_ref[1, 0] = jnp.where(ocean, sea, air)
    partner_ref[...] = partner_in_ref[...]


def shards(
    state,
    courant,
    mixing,
    exchange_coef,
    sea_mask,
    margin_count,
    margin_row,
    margin_col,
    margin_weight,
):
    fields, levels, rows, cols = state.shape
    slots = margin_row.shape[-1]
    comp_total = lax.axis_size("comp")
    tile_total = lax.axis_size("tile")
    half = rows // 2
    edge = cols // 4
    lists = (3, comp_total, slots)
    hbm = pl.BlockSpec(memory_space=pl.ANY)
    partner, halo = pl.pallas_call(
        functools.partial(
            exchange_kernel, rows, cols, slots, comp_total, tile_total, fields * levels
        ),
        out_shape=(
            jax.ShapeDtypeStruct((fields, rows, cols), jnp.float32),
            jax.ShapeDtypeStruct((2, rows, LANES), jnp.float32),
        ),
        in_specs=[
            pl.BlockSpec(memory_space=pl.ANY),
            pl.BlockSpec(memory_space=pltpu.SMEM),
            hbm,
            hbm,
            hbm,
        ],
        out_specs=(hbm, hbm),
        scratch_shapes=[
            pltpu.VMEM(lists, jnp.int32),
            pltpu.VMEM(lists, jnp.int32),
            pltpu.VMEM(lists, jnp.float32),
            pltpu.VMEM((fields, rows, cols), jnp.float32),
            pltpu.VMEM((fields, rows, cols), jnp.float32),
            pltpu.VMEM((2, fields, levels, rows, LANES), jnp.float32),
            pltpu.VMEM((2 * fields * rows, cols), jnp.bfloat16),
            pltpu.VMEM((2, 2 * fields * half, 2 * edge), jnp.bfloat16),
            pltpu.VMEM((3, comp_total, fields, slots), jnp.float32),
            pltpu.VMEM((3, comp_total, fields, slots), jnp.float32),
            pltpu.VMEM((2, rows, LANES), jnp.float32),
            pltpu.VMEM((2 * fields * rows, cols), jnp.float32),
            pltpu.VMEM((2, 2 * fields * half, 2 * edge), jnp.float32),
            pltpu.VMEM((cols, LANES), jnp.bfloat16),
            pltpu.VMEM((fields, rows, cols), jnp.float32),
            pltpu.VMEM(lists, jnp.int32),
            pltpu.VMEM(lists, jnp.int32),
            pltpu.VMEM(lists, jnp.float32),
            pltpu.VMEM((2 * fields * rows, cols), jnp.bfloat16),
            pltpu.VMEM((2, 2 * fields * half, 2 * edge), jnp.bfloat16),
            pltpu.VMEM((fields, rows, cols), jnp.float32),
            pltpu.VMEM((fields, rows, cols), jnp.float32),
            pltpu.SemaphoreType.DMA((6,)),
            pltpu.SemaphoreType.DMA((3, comp_total)),
            pltpu.SemaphoreType.DMA((3, comp_total)),
            pltpu.SemaphoreType.DMA((2,)),
            pltpu.SemaphoreType.DMA((2,)),
            pltpu.SemaphoreType.DMA((5,)),
            pltpu.SemaphoreType.DMA((5,)),
        ],
        compiler_params=pltpu.CompilerParams(
            collective_id=0, has_side_effects=True, vmem_limit_bytes=VMEM_BYTES
        ),
    )(
        state,
        margin_count.reshape(3, 1, comp_total),
        margin_row.reshape(lists),
        margin_col.reshape(lists),
        margin_weight.reshape(lists),
    )
    block = 16
    plane = pl.BlockSpec((block, cols), lambda i: (i, 0))
    return pl.pallas_call(
        advance_kernel,
        grid=(rows // block,),
        out_shape=(
            jax.ShapeDtypeStruct(state.shape, jnp.float32),
            jax.ShapeDtypeStruct((fields, rows, cols), jnp.float32),
        ),
        in_specs=[
            pl.BlockSpec((fields, levels, block, cols), lambda i: (0, 0, i, 0)),
            pl.BlockSpec(courant.shape, lambda i: (0, 0)),
            pl.BlockSpec(mixing.shape, lambda i: (0, 0)),
            plane,
            plane,
            pl.BlockSpec((2, block, LANES), lambda i: (0, i, 0)),
            pl.BlockSpec((fields, block, cols), lambda i: (0, i, 0)),
        ],
        out_specs=(
            pl.BlockSpec((fields, levels, block, cols), lambda i: (0, 0, i, 0)),
            pl.BlockSpec((fields, block, cols), lambda i: (0, i, 0)),
        ),
        scratch_shapes=[
            pltpu.VMEM((rows, levels), jnp.float32),
            pltpu.VMEM((rows, levels - 1), jnp.float32),
        ],
    )(state, courant, mixing, exchange_coef, sea_mask, halo, partner)


def solution(mesh):
    in_specs = (
        P(None, None, "comp", "tile"),
        P(None, "comp"),
        P(None, "comp"),
        P("comp", "tile"),
        P("comp", "tile"),
        P("comp", "tile", None, None),
        P("comp", "tile", None, None, None),
        P("comp", "tile", None, None, None),
        P("comp", "tile", None, None, None),
    )
    out_specs = (P(None, None, "comp", "tile"), P(None, "comp", "tile"))
    return jax.shard_map(shards, mesh=mesh, in_specs=in_specs, out_specs=out_specs, check_vma=False)
```

```python
import functools

import jax
import jax.numpy as jnp
from jax import lax
from jax.experimental import pallas as pl
from jax.experimental.pallas import tpu as pltpu
from jax.sharding import PartitionSpec as P

SUBSTEPS = 2
LANES = 128
MESH = pl.DeviceIdType.MESH
SHIFT = 256
VMEM_BYTES = 67043328


def chunk_of(slot_count):
    for width in (2048, 1024, 512, 256):
        if slot_count % width == 0:
            return width
    return slot_count


def one_hot(iota_ref, key, depth):
    width = key.shape[1]
    shifted = (key - SHIFT).astype(jnp.float32)
    wide = jnp.broadcast_to(shifted, (16, width)).astype(jnp.bfloat16)
    one = jnp.ones((16, width), jnp.bfloat16)
    zero = jnp.zeros((16, width), jnp.bfloat16)
    parts = []
    for start in range(0, depth, 16):
        number = iota_ref[start : start + 16, :]
        number = jnp.concatenate([number] * (width // LANES), axis=1)
        parts.append(jnp.where(wide == number, one, zero))
    return jnp.concatenate(parts, axis=0)


def split(values):
    high = values.astype(jnp.bfloat16)
    low = (values - high.astype(jnp.float32)).astype(jnp.bfloat16)
    return high, low


def keys_of(which, row, col, row_count, col_count):
    if which == 1:
        return col, row
    half = row_count // 2
    edge = col_count // 4
    base = 0 if which == 0 else col_count - edge
    upper = (row >= half).astype(jnp.int32)
    return upper * edge + (col - base), row - upper * half


def exchange_kernel(
    row_count,
    col_count,
    slot_count,
    comp_total,
    tile_total,
    fl_count,
    state_ref,
    count_ref,
    row_hbm,
    col_hbm,
    weight_hbm,
    partner_hbm,
    halo_ref,
    row_ref,
    col_ref,
    weight_ref,
    partner_ref,
    surface,
    edges,
    table_mid,
    table_side,
    outgoing,
    incoming,
    halo_out,
    total_mid,
    total_side,
    iota_ref,
    far_surface,
    far_row,
    far_col,
    far_weight,
    far_mid,
    far_side,
    share_out,
    share_in,
    load_sem,
    send_sem,
    recv_sem,
    halo_send_sem,
    halo_recv_sem,
    far_send_sem,
    far_recv_sem,
):
    comp = lax.axis_index("comp")
    tile = lax.axis_index("tile")
    sea = comp_total - 1
    aide = comp_total - 2
    ocean = comp == sea
    helper = comp == aide
    tiles = [lax.rem(tile + offset + tile_total, tile_total) for offset in (-1, 0, 1)]
    fields = surface.shape[0]
    half = row_count // 2
    edge = col_count // 4
    width = chunk_of(slot_count)
    chunks = slot_count // width
    low_list = jnp.where(ocean, 0, sea)
    high_list = jnp.where(ocean, aide, comp_total)
    low_greet = jnp.where(helper, sea, low_list)
    high_greet = jnp.where(helper, sea, high_list)

    load_surface = pltpu.make_async_copy(state_ref.at[:, 0], surface, load_sem.at[0])
    load_surface.start()
    list_loads = []
    for place, (source, target) in enumerate(
        ((row_hbm, row_ref), (col_hbm, col_ref), (weight_hbm, weight_ref))
    ):
        load = pltpu.make_async_copy(source, target, load_sem.at[3 + place])
        load.start()
        list_loads.append(load)
    loads = []
    for side, start in ((0, 0), (1, col_count - LANES)):
        load = pltpu.make_async_copy(
            state_ref.at[:, :, :, pl.ds(start, LANES)], edges.at[side], load_sem.at[1 + side]
        )
        load.start()
        loads.append(load)

    barrier = pltpu.get_barrier_semaphore()
    for which in (0, 2):
        pl.semaphore_signal(barrier, inc=1, device_id=(comp, tiles[which]), device_id_type=MESH)

    def greet(other, carry):
        for which in range(3):
            pl.semaphore_signal(
                barrier, inc=1, device_id=(other, tiles[which]), device_id_type=MESH
            )
        return carry

    lax.fori_loop(low_greet, high_greet, greet, 0)

    @pl.when(ocean)
    def _():
        pl.semaphore_signal(barrier, inc=1, device_id=(aide, tile), device_id_type=MESH)

    @pl.when(helper)
    def _():
        pl.semaphore_signal(barrier, inc=1, device_id=(sea, tile), device_id_type=MESH)

    iota_ref[...] = (lax.broadcasted_iota(jnp.int32, iota_ref.shape, 0) - SHIFT).astype(
        jnp.float32
    ).astype(jnp.bfloat16)
    load_surface.wait()

    def build_tables(source, mid, side_tables):
        for field in range(fields):
            high, low = split(source[field])
            for index, piece in ((field, high), (fields + field, low)):
                mid[index * row_count : (index + 1) * row_count, :] = piece
                for side, base in ((0, 0), (1, col_count - edge)):
                    side_tables[side, index * half : (index + 1) * half, :] = jnp.concatenate(
                        [piece[:half, base : base + edge], piece[half:, base : base + edge]],
                        axis=1,
                    )

    build_tables(surface, table_mid, table_side)
    def clear_totals():
        total_mid[...] = jnp.zeros_like(total_mid)
        total_side[...] = jnp.zeros_like(total_side)

    clear_totals()
    for load in loads:
        load.wait()
    lane = lax.broadcasted_iota(jnp.int32, (row_count, LANES), 1)
    for side in range(2):
        packed = jnp.zeros((row_count, LANES), jnp.float32)
        for place in range(fl_count):
            level = edges[side, place // (fl_count // fields), place % (fl_count // fields)]
            shift = SUBSTEPS * place + (0 if side == 0 else SUBSTEPS)
            moved = level if shift == 0 else pltpu.roll(level, shift, 1)
            packed = jnp.where(lane // SUBSTEPS == place, moved, packed)
        halo_out[side] = packed
    for load in list_loads:
        load.wait()
    pl.semaphore_wait(
        barrier,
        2 + 3 * (high_greet - low_greet) + jnp.where(ocean | helper, 1, 0),
    )

    far_copies = []
    for place, (source, target) in enumerate(
        (
            (surface, far_surface),
            (row_ref, far_row),
            (col_ref, far_col),
            (weight_ref, far_weight),
        )
    ):
        far_copies.append(
            pltpu.make_async_remote_copy(
                src_ref=source,
                dst_ref=target,
                send_sem=far_send_sem.at[place],
                recv_sem=far_recv_sem.at[place],
                device_id=(aide, tile),
                device_id_type=MESH,
            )
        )
    share_copy = pltpu.make_async_remote_copy(
        src_ref=share_out,
        dst_ref=share_in,
        send_sem=far_send_sem.at[4],
        recv_sem=far_recv_sem.at[4],
        device_id=(sea, tile),
        device_id_type=MESH,
    )

    @pl.when(ocean)
    def _():
        for copy in far_copies:
            copy.start()

    def copy_of(which, other):
        return pltpu.make_async_remote_copy(
            src_ref=outgoing.at[which, other],
            dst_ref=incoming.at[2 - which, comp],
            send_sem=send_sem.at[which, other],
            recv_sem=recv_sem.at[2 - which, comp],
            device_id=(jnp.where(helper, aide, other), tiles[which]),
            device_id_type=MESH,
        )

    def aide_copy(which):
        return pltpu.make_async_remote_copy(
            src_ref=outgoing.at[which, aide],
            dst_ref=incoming.at[2 - which, sea],
            send_sem=send_sem.at[which, aide],
            recv_sem=recv_sem.at[2 - which, sea],
            device_id=(aide, tiles[which]),
            device_id_type=MESH,
        )

    def own_copy(place, source, target):
        return pltpu.make_async_copy(
            outgoing.at[1, source], incoming.at[1, target], load_sem.at[3 + place]
        )

    def landing_of(which, other):
        return pltpu.make_async_remote_copy(
            src_ref=outgoing.at[which, other],
            dst_ref=incoming.at[which, other],
            send_sem=send_sem.at[which, other],
            recv_sem=recv_sem.at[which, other],
            device_id=(other, tiles[which]),
            device_id_type=MESH,
        )

    def pick_lists(other, rows_of, cols_of, mid, side_tables, masked):
        def pick_chunk(piece, inner):
            start = pl.multiple_of(piece * width, width)
            span = pl.ds(start, width)
            live_slot = lax.broadcasted_iota(jnp.int32, (1, width), 1) + start
            for which in (1, 0, 2):
                row = rows_of[which, pl.ds(other, 1), span]
                col = cols_of[which, pl.ds(other, 1), span]
                key, inside = keys_of(which, row, col, row_count, col_count)
                if which == 1:
                    table, depth, rows = mid[...], col_count, row_count
                else:
                    table, depth, rows = side_tables[which // 2], 2 * edge, half
                picked = jnp.dot(
                    table, one_hot(iota_ref, key, depth), preferred_element_type=jnp.float32
                )
                match = lax.broadcasted_iota(jnp.int32, (rows, width), 0) == inside
                if masked:
                    live = live_slot < count_ref[which, 0, other]
                for field in range(fields):
                    both = (
                        picked[field * rows : (field + 1) * rows]
                        + picked[(fields + field) * rows : (fields + field + 1) * rows]
                    )
                    value = jnp.sum(jnp.where(match, both, 0.0), axis=0, keepdims=True)
                    if masked:
                        value = jnp.where(live, value, 0.0)
                    outgoing[which, other, field : field + 1, span] = value
            return inner

        lax.fori_loop(0, chunks, pick_chunk, 0)

    def pick(other, carry):
        pick_lists(other, row_ref, col_ref, table_mid, table_side, True)
        for which in (0, 2):
            copy_of(which, other).start()

        @pl.when(jnp.logical_not(helper))
        def _():
            copy_of(1, other).start()

        return carry

    lax.fori_loop(low_list, high_list, pick, 0)

    @pl.when(helper)
    def _():
        own_copy(0, sea, aide).start()
        for copy in far_copies:
            copy.wait_recv()
        build_tables(far_surface, far_mid, far_side)
        pick_lists(aide, far_row, far_col, far_mid, far_side, False)
        for which in (0, 2):
            aide_copy(which).start()
        own_copy(1, aide, sea).start()

    def halo_copy(side):
        return pltpu.make_async_remote_copy(
            src_ref=halo_out.at[side],
            dst_ref=halo_ref.at[1 - side],
            send_sem=halo_send_sem.at[side],
            recv_sem=halo_recv_sem.at[1 - side],
            device_id=(comp, tiles[2 * side]),
            device_id_type=MESH,
        )

    for side in range(2):
        halo_copy(side).start()

    def land_lists(other, rows_of, cols_of, weights_of, masked):
        def land_chunk(piece, inner):
            start = pl.multiple_of(piece * width, width)
            span = pl.ds(start, width)
            live_slot = lax.broadcasted_iota(jnp.int32, (1, width), 1) + start
            for which in (1, 0, 2):
                row = rows_of[which, pl.ds(other, 1), span]
                col = cols_of[which, pl.ds(other, 1), span]
                key, inside = keys_of(which, row, col, row_count, col_count)
                depth, rows = (col_count, row_count) if which == 1 else (2 * edge, half)
                term = incoming[which, other, :, span] * weights_of[which, pl.ds(other, 1), span]
                if masked:
                    term = jnp.where(live_slot < count_ref[which, 0, other], term, 0.0)
                high, low = split(term)
                wide_key = jnp.broadcast_to(
                    inside.astype(jnp.float32) - SHIFT, (16, width)
                ).astype(jnp.bfloat16)
                zero = jnp.zeros((16, width), jnp.bfloat16)
                parts = []
                matches = []
                for first in range(0, rows, 16):
                    number = iota_ref[first : first + 16, :]
                    number = jnp.concatenate([number] * (width // LANES), axis=1)
                    matches.append(wide_key == number)
                for piece_of in (high, low):
                    for field in range(fields):
                        value = jnp.broadcast_to(
                            piece_of[field : field + 1].astype(jnp.float32), (16, width)
                        ).astype(jnp.bfloat16)
                        for match in matches:
                            parts.append(jnp.where(match, value, zero))
                spread = jnp.concatenate(parts, axis=0)
                added = lax.dot_general(
                    spread,
                    one_hot(iota_ref, key, depth),
                    (((1,), (1,)), ((), ())),
                    preferred_element_type=jnp.float32,
                )
                if which == 1:
                    total_mid[...] += added
                else:
                    total_side[which // 2] += added
            return inner

        lax.fori_loop(0, chunks, land_chunk, 0)

    def land(other, carry):
        for which in (0, 2):
            landing_of(which, other).wait_recv()

        @pl.when(jnp.logical_not(helper))
        def _():
            landing_of(1, other).wait_recv()

        land_lists(other, row_ref, col_ref, weight_ref, True)
        return carry

    def gather_totals(field, target):
        first, second = field, fields + field
        target[field] = (
            total_mid[first * row_count : (first + 1) * row_count, :]
            + total_mid[second * row_count : (second + 1) * row_count, :]
        )
        for side, base in ((0, 0), (1, col_count - edge)):
            extra = (
                total_side[side, first * half : (first + 1) * half, :]
                + total_side[side, second * half : (second + 1) * half, :]
            )
            target[field, :half, base : base + edge] += extra[:, :edge]
            target[field, half:, base : base + edge] += extra[:, edge:]

    @pl.when(helper)
    def _():
        own_copy(0, sea, aide).wait()
        for which in (0, 2):
            landing_of(which, aide).wait_recv()
        land_lists(aide, far_row, far_col, far_weight, False)
        for field in range(fields):
            gather_totals(field, share_out)
        share_copy.start()
        clear_totals()
        own_copy(1, aide, sea).wait()

    lax.fori_loop(low_list, high_list, land, 0)

    for field in range(fields):
        gather_totals(field, partner_ref)

    @pl.when(ocean)
    def _():
        share_copy.wait_recv()
        partner_ref[...] += share_in[...]

    for field in range(fields):
        pltpu.make_async_copy(
            partner_ref.at[field], partner_hbm.at[field], load_sem.at[field]
        ).start()

    def finish(other, carry):
        for which in (0, 2):
            copy_of(which, other).wait_send()

        @pl.when(jnp.logical_not(helper))
        def _():
            copy_of(1, other).wait_send()

        return carry

    lax.fori_loop(low_list, high_list, finish, 0)

    @pl.when(helper)
    def _():
        for which in (0, 2):
            aide_copy(which).wait_send()
        share_copy.wait_send()

    @pl.when(ocean)
    def _():
        for copy in far_copies:
            copy.wait_send()

    for side in range(2):
        copy = halo_copy(side)
        copy.wait_send()
    for side in range(2):
        halo_copy(1 - side).wait_recv()
    for field in range(fields):
        pltpu.make_async_copy(
            partner_ref.at[field], partner_hbm.at[field], load_sem.at[field]
        ).wait()


def advance_kernel(
    state_ref,
    courant_ref,
    mixing_ref,
    exchange_ref,
    sea_ref,
    halo_ref,
    partner_in_ref,
    new_ref,
    partner_ref,
    speed_ref,
    mix_ref,
):
    fields, levels, rows, cols = state_ref.shape
    step = pl.program_id(0)
    ocean = lax.axis_index("comp") == lax.axis_size("comp") - 1

    @pl.when(step == 0)
    def _():
        speed_ref[...] = jnp.transpose(courant_ref[...])
        mix_ref[...] = jnp.transpose(mixing_ref[...])

    span = pl.ds(pl.multiple_of(step * rows, rows), rows)
    total = cols + LANES
    lane = lax.broadcasted_iota(jnp.int32, (rows, LANES), 1)
    speeds = speed_ref[span, :]
    mixes = mix_ref[span, :]
    surface = []
    for field in range(fields):
        columns = []
        for level in range(levels):
            place = field * levels + level
            east = halo_ref[1]
            east = east if place == 0 else pltpu.roll(east, LANES - SUBSTEPS * place, 1)
            west = pltpu.roll(halo_ref[0], LANES - SUBSTEPS * (place + 1), 1)
            ends = jnp.where(lane < LANES // 2, east, west)
            columns.append(jnp.concatenate([state_ref[field, level], ends], axis=1))
        for substep in range(SUBSTEPS):
            span_out = total if substep < SUBSTEPS - 1 else cols
            moved = []
            for level in range(levels):
                q = columns[level]
                left = pltpu.roll(q, 1, 1)[:, :span_out]
                right = pltpu.roll(q, total - 1, 1)[:, :span_out]
                c = speeds[:, level : level + 1]
                half_c = 0.5 * c
                half_square = half_c * c
                from_left = jnp.broadcast_to(half_c + half_square, (rows, span_out))
                from_right = jnp.broadcast_to(half_square - half_c, (rows, span_out))
                own = jnp.broadcast_to(1.0 - 2.0 * half_square, (rows, span_out))
                moved.append(own * q[:, :span_out] + from_left * left + from_right * right)
            columns = []
            flux = None
            for level in range(levels):
                value = moved[level]
                if level < levels - 1:
                    m = jnp.broadcast_to(mixes[:, level : level + 1], (rows, span_out))
                    above = m * (moved[level + 1] - moved[level])
                    value = value + above
                if level > 0:
                    value = value - flux
                if level < levels - 1:
                    flux = above
                columns.append(value)
        for level in range(1, levels):
            new_ref[field, level] = columns[level]
        surface.append(columns[0])
    rate = exchange_ref[...] * sea_ref[...].astype(jnp.float32)
    first, second = surface
    far = partner_in_ref[0]
    far_second = partner_in_ref[1]
    new_ref[0, 0] = first + rate * (far - first)
    air = second + rate * (1.2 * far - 0.3 * far_second - second)
    sea = second + rate * (1.2 * first - far_second)
    new_ref[1, 0] = jnp.where(ocean, sea, air)
    partner_ref[...] = partner_in_ref[...]


def shards(
    state,
    courant,
    mixing,
    exchange_coef,
    sea_mask,
    margin_count,
    margin_row,
    margin_col,
    margin_weight,
):
    fields, levels, rows, cols = state.shape
    slots = margin_row.shape[-1]
    comp_total = lax.axis_size("comp")
    tile_total = lax.axis_size("tile")
    half = rows // 2
    edge = cols // 4
    lists = (3, comp_total, slots)
    hbm = pl.BlockSpec(memory_space=pl.ANY)
    partner, halo = pl.pallas_call(
        functools.partial(
            exchange_kernel, rows, cols, slots, comp_total, tile_total, fields * levels
        ),
        out_shape=(
            jax.ShapeDtypeStruct((fields, rows, cols), jnp.float32),
            jax.ShapeDtypeStruct((2, rows, LANES), jnp.float32),
        ),
        in_specs=[
            pl.BlockSpec(memory_space=pl.ANY),
            pl.BlockSpec(memory_space=pltpu.SMEM),
            hbm,
            hbm,
            hbm,
        ],
        out_specs=(hbm, hbm),
        scratch_shapes=[
            pltpu.VMEM(lists, jnp.int32),
            pltpu.VMEM(lists, jnp.int32),
            pltpu.VMEM(lists, jnp.float32),
            pltpu.VMEM((fields, rows, cols), jnp.float32),
            pltpu.VMEM((fields, rows, cols), jnp.float32),
            pltpu.VMEM((2, fields, levels, rows, LANES), jnp.float32),
            pltpu.VMEM((2 * fields * rows, cols), jnp.bfloat16),
            pltpu.VMEM((2, 2 * fields * half, 2 * edge), jnp.bfloat16),
            pltpu.VMEM((3, comp_total, fields, slots), jnp.float32),
            pltpu.VMEM((3, comp_total, fields, slots), jnp.float32),
            pltpu.VMEM((2, rows, LANES), jnp.float32),
            pltpu.VMEM((2 * fields * rows, cols), jnp.float32),
            pltpu.VMEM((2, 2 * fields * half, 2 * edge), jnp.float32),
            pltpu.VMEM((cols, LANES), jnp.bfloat16),
            pltpu.VMEM((fields, rows, cols), jnp.float32),
            pltpu.VMEM(lists, jnp.int32),
            pltpu.VMEM(lists, jnp.int32),
            pltpu.VMEM(lists, jnp.float32),
            pltpu.VMEM((2 * fields * rows, cols), jnp.bfloat16),
            pltpu.VMEM((2, 2 * fields * half, 2 * edge), jnp.bfloat16),
            pltpu.VMEM((fields, rows, cols), jnp.float32),
            pltpu.VMEM((fields, rows, cols), jnp.float32),
            pltpu.SemaphoreType.DMA((6,)),
            pltpu.SemaphoreType.DMA((3, comp_total)),
            pltpu.SemaphoreType.DMA((3, comp_total)),
            pltpu.SemaphoreType.DMA((2,)),
            pltpu.SemaphoreType.DMA((2,)),
            pltpu.SemaphoreType.DMA((5,)),
            pltpu.SemaphoreType.DMA((5,)),
        ],
        compiler_params=pltpu.CompilerParams(
            collective_id=0, has_side_effects=True, vmem_limit_bytes=VMEM_BYTES
        ),
    )(
        state,
        margin_count.reshape(3, 1, comp_total),
        margin_row.reshape(lists),
        margin_col.reshape(lists),
        margin_weight.reshape(lists),
    )
    block = 16
    plane = pl.BlockSpec((block, cols), lambda i: (i, 0))
    return pl.pallas_call(
        advance_kernel,
        grid=(rows // block,),
        out_shape=(
            jax.ShapeDtypeStruct(state.shape, jnp.float32),
            jax.ShapeDtypeStruct((fields, rows, cols), jnp.float32),
        ),
        in_specs=[
            pl.BlockSpec((fields, levels, block, cols), lambda i: (0, 0, i, 0)),
            pl.BlockSpec(courant.shape, lambda i: (0, 0)),
            pl.BlockSpec(mixing.shape, lambda i: (0, 0)),
            plane,
            plane,
            pl.BlockSpec((2, block, LANES), lambda i: (0, i, 0)),
            pl.BlockSpec((fields, block, cols), lambda i: (0, i, 0)),
        ],
        out_specs=(
            pl.BlockSpec((fields, levels, block, cols), lambda i: (0, 0, i, 0)),
            pl.BlockSpec((fields, block, cols), lambda i: (0, i, 0)),
        ),
        scratch_shapes=[
            pltpu.VMEM((rows, levels), jnp.float32),
            pltpu.VMEM((rows, levels - 1), jnp.float32),
        ],
    )(state, courant, mixing, exchange_coef, sea_mask, halo, partner)


def solution(mesh):
    in_specs = (
        P(None, None, "comp", "tile"),
        P(None, "comp"),
        P(None, "comp"),
        P("comp", "tile"),
        P("comp", "tile"),
        P("comp", "tile", None, None),
        P("comp", "tile", None, None, None),
        P("comp", "tile", None, None, None),
        P("comp", "tile", None, None, None),
    )
    out_specs = (P(None, None, "comp", "tile"), P(None, "comp", "tile"))
    return jax.shard_map(shards, mesh=mesh, in_specs=in_specs, out_specs=out_specs, check_vma=False)
```
